32 devices in a mesh: groups: 2 (over y), section: 2 (over x), expert: 4 (over z), pair: 2 (over core).
Axes of the slice: x: 2, y: 2, z: 4, core: 2. Of those that a mesh axis runs over, the one named last changes fastest.
Arguments:
- transit_activation: bfloat16 [2, 32, 3072], P('section', ('groups', 'expert', 'pair')), parts along dimension 1, may hold values from -6 to 6
- incoming_queue: bfloat16 [2, 32, 3072], P('section', ('groups', 'expert', 'pair')), parts along dimension 1, may hold values from -6 to 6
- expert_assignment: int32 [2, 3, 32, 1], P('section', None, ('groups', 'expert', 'pair')), parts along dimension 2, may hold values from 0 to 1; in each aligned block of 2 rows (0 to 1, 2 to 3, ..., all dimensions but the last counted through in order) at most 2 rows name the same one
- rescale_factor: float32 [2, 3072], P('section'), may hold values from 0.25 to 1.75
- routing_matrix: bfloat16 [2, 3072, 2], P('section'), may hold values from -0.109375 to 0.109375
- gating_matrix: bfloat16 [2, 2, 3072, 8192], P('section', 'pair', None, 'expert'), may hold values from -0.109375 to 0.109375
- expand_matrix: bfloat16 [2, 2, 3072, 8192], P('section', 'pair', None, 'expert'), may hold values from -0.109375 to 0.109375
- contract_matrix: bfloat16 [2, 2, 8192, 3072], P('section', 'pair', 'expert'), may hold values from -0.0625 to 0.0625
Outputs:
- inflight_out: bfloat16 [2, 32, 3072], P('section', ('groups', 'expert', 'pair')), parts along dimension 1
- finished: bfloat16 [2, 32, 3072], P('section', ('groups', 'expert', 'pair')), parts along dimension 1
The draws below stay inside these ranges and needn't reach their ends.
There are 2 independent parts, one for each index of `groups`. The reference program is written for one: setup_inputs(seed, part) draws one part's arguments, and reference() takes and returns one part's arrays. A program takes and returns all parts, laid end to end along the dimension named above; an argument that names none is the same for every part. Nothing has to cross between parts.
Inputs may be any that keep to these rules, and one draw needn't show every extreme that they name: `expert_assignment`: the expert chosen by each token of each layer and tick. In each aligned block of 2 rows, no expert is chosen by more than 2 rows.
All inputs are finite; a program needn't handle non-finite values.
Results may differ from the reference program's by a relative error of at most 0.023.
Values may be sent and summed in bfloat16 or wider, within the bound.
No kernel may reach another device: no remote copies, remote signals or barrier semaphores. Data moves between devices by JAX's collectives and lax.ppermute only.
A program may use at most 64 MiB of HBM per device.

```python
import math
import jax
import jax.numpy as jnp
import numpy as np
from jax import lax

EMBED_DIMENSION = 3072
FF = 8192
EXPERTS = 2
TICKS = 3
TOK_DEV = 2
MICRO_COUNT = 16
CAP = 2
N_SECTION = 2
N_EXPERT = 4
N_PAIR = 2


def steps_of(own_key, dims, cuts, low, largest):
    def one(position, blocks):
        steps = jax.random.uniform(jax.random.fold_in(jax.random.fold_in(own_key, 6), position), (blocks,), jnp.float32, low / len(cuts), largest / len(cuts))
        return jnp.repeat(jnp.exp(steps), dims[position] // blocks).reshape((-1,) + (1,) * (len(dims) - position - 1))

    level = one(*cuts[0])
    for cut in cuts[1:]:
        level = level * one(*cut)
    return level


def assign_block(rng, own, number, rows, count, top, reach, lean):
    ranking = jax.random.permutation(rng, count)
    packed, common = shares(count, rows * top, reach, lean, True), shares(count, rows * top, reach, lean, False)
    places = jnp.arange(count)

    def named(sizes, rotation):
        used = int((sizes > 0).sum())
        fixed = max(1, used // 4)
        moved = fixed + (places - fixed + rotation * (used - fixed)) % max(1, count - fixed)
        return jnp.zeros((count,), jnp.int32).at[ranking[jnp.where(places < fixed, places, moved)]].set(jnp.asarray(sizes, jnp.int32))

    sizes = jnp.where(number % 4 == 0, named(packed, number // 4), named(common, number - number // 4 - 1))
    mixed = jax.random.permutation(jax.random.fold_in(own, 3), count)
    giver, sink = mixed[0:count // 2 * 2:2], mixed[1:count // 2 * 2:2]
    room = jnp.minimum(sizes[giver] - 1, reach - sizes[sink]) // 2
    room = jnp.where((giver == ranking[0]) | (sink == ranking[0]) | (sizes[sink] == 0), 0, jnp.maximum(room, 0))
    moved = jax.random.randint(jax.random.fold_in(own, 4), (count // 2,), 0, 1 << 20) % (room + 1)
    sizes = sizes.at[giver].add(-moved).at[sink].add(moved)
    members = jnp.searchsorted(jnp.cumsum(sizes), jnp.arange(rows * top), side="right").astype(jnp.int32)
    grid = members.reshape(top, rows).T
    grid = grid[jax.random.permutation(jax.random.fold_in(own, 1), rows)]
    rotation = jax.random.randint(jax.random.fold_in(own, 2), (rows, 1), 0, top)
    return jnp.take_along_axis(grid, (jnp.arange(top)[None, :] + rotation) % top, axis=1)


def shares(number_of, total, bound, skew, full):
    portions = [(1 << 20) // math.isqrt(grade ** skew) + 1 for grade in range(1, number_of + 1)]
    largest = bound if full else min(bound, max(-(-total // number_of), total * portions[0] // sum(portions)))
    least = 1 if total - largest >= number_of - 1 else 0
    counts, spare = [largest] + [least] * (number_of - 1), total - largest - least * (number_of - 1)
    while spare > 0:
        candidates = [i for i in range(1, number_of) if counts[i] < largest] or [i for i in range(1, number_of) if counts[i] < bound]
        pool, budget = sum([portions[i] for i in candidates]), spare
        for i in candidates:
            extra = min(bound - counts[i], max(1, budget * portions[i] // pool), spare)
            counts[i] = counts[i] + extra
            spare = spare - extra
    return np.array(counts)


def centred(rng, dims, scale, bound, cuts=(), kind=jnp.bfloat16):
    drawn = scale * jax.random.normal(rng, dims, jnp.float32)
    if cuts:
        drawn = drawn * steps_of(rng, dims, cuts, -0.22, 0.18)
    return jnp.clip(drawn, -bound, bound).astype(kind)


def setup_inputs(seed: int = 0, part: int = 0) -> dict:
    keys = jax.random.split(jax.random.key(seed), 9)
    part_keys = jax.random.split(jax.random.fold_in(keys[8], part), 9)
    transit_activation = centred(part_keys[0], (N_SECTION, MICRO_COUNT, EMBED_DIMENSION), 1.0, 6.0, ((0, 2), (1, 8)))
    incoming_queue = centred(part_keys[1], (N_SECTION, MICRO_COUNT, EMBED_DIMENSION), 1.0, 6.0, ((0, 2), (1, 8)))
    expert_assignment_keys = jax.random.split(jax.random.fold_in(part_keys[2], 1), N_SECTION * TICKS * MICRO_COUNT // TOK_DEV)
    expert_assignment_turns = jax.random.permutation(jax.random.fold_in(part_keys[2], 3), N_SECTION * TICKS * MICRO_COUNT // TOK_DEV)
    expert_assignment = jax.vmap(lambda own, number: assign_block(jax.random.fold_in(part_keys[2], 2), own, number, TOK_DEV, EXPERTS, 1, CAP, 2))(expert_assignment_keys, expert_assignment_turns).reshape((N_SECTION, TICKS, MICRO_COUNT, 1))
    rescale_factor = jnp.clip(1.0 + 0.15 * jax.random.normal(keys[3], (N_SECTION, EMBED_DIMENSION), jnp.float32), 0.25, 1.75)
    routing_matrix = centred(keys[4], (N_SECTION, EMBED_DIMENSION, EXPERTS), EMBED_DIMENSION ** -0.5, 0.109375, ((0, 2),))
    gating_matrix = centred(keys[5], (N_SECTION, EXPERTS, EMBED_DIMENSION, FF), EMBED_DIMENSION ** -0.5, 0.109375, ((0, 2), (1, 2), (3, 4)))
    expand_matrix = centred(keys[6], (N_SECTION, EXPERTS, EMBED_DIMENSION, FF), EMBED_DIMENSION ** -0.5, 0.109375, ((0, 2), (1, 2), (3, 4)))
    contract_matrix = centred(keys[7], (N_SECTION, EXPERTS, FF, EMBED_DIMENSION), FF ** -0.5, 0.0625, ((0, 2), (1, 2), (2, 4)))
    return dict(transit_activation=transit_activation, incoming_queue=incoming_queue, expert_assignment=expert_assignment, rescale_factor=rescale_factor, routing_matrix=routing_matrix, gating_matrix=gating_matrix, expand_matrix=expand_matrix, contract_matrix=contract_matrix)


def down_sum(hidden, down):
    part = FF // N_EXPERT

    def add(index, total):
        start = index.astype(jnp.int32) * part
        columns = lax.dynamic_slice_in_dim(hidden, start, part, 1)
        weights = lax.dynamic_slice_in_dim(down, start, part, 0)
        piece = jnp.dot(columns, weights, preferred_element_type=jnp.float32)
        return total + lax.optimization_barrier(piece.astype(jnp.bfloat16)).astype(jnp.float32)
    return lax.fori_loop(0, N_EXPERT, add, jnp.zeros((hidden.shape[0], EMBED_DIMENSION), jnp.float32))

def layer_apply(rows, picks, gain, table, gate_all, up_all, down_all):
    sources = N_EXPERT * N_PAIR
    wide = rows.astype(jnp.float32)
    square = lax.optimization_barrier(jnp.mean(wide * wide, axis=-1, keepdims=True))
    normed = (wide * lax.rsqrt(square + 1e-06) * gain).astype(jnp.bfloat16)
    logits = jnp.dot(normed, table, preferred_element_type=jnp.float32)
    chosen = jnp.take_along_axis(logits, picks, axis=1)[:, 0]
    other = jnp.take_along_axis(logits, (1 - picks).astype(jnp.int32), axis=1)[:, 0]
    weight = jax.nn.sigmoid(chosen - other)[:, None]
    pick = picks[:, 0].astype(jnp.int32)
    blocks = pick.reshape(sources, TOK_DEV)
    flags = (blocks[:, :, None] == jnp.arange(EXPERTS, dtype=jnp.int32)[None, None, :]).astype(jnp.int32)
    before = (jnp.cumsum(flags, axis=1) - flags).astype(jnp.int32)
    slot = lax.optimization_barrier(jnp.sum(before * flags, axis=-1)).reshape(-1).astype(jnp.int32)
    source = (jnp.arange(MICRO_COUNT, dtype=jnp.int32) // TOK_DEV).astype(jnp.int32)
    buffer = jnp.zeros((EXPERTS, sources, CAP, EMBED_DIMENSION), jnp.bfloat16).at[pick, source, slot].set(normed)
    answers = []
    for expert in range(EXPERTS):
        flat = buffer[expert].reshape(sources * CAP, EMBED_DIMENSION)
        gate = jnp.dot(flat, gate_all[expert], preferred_element_type=jnp.float32)
        upper = jnp.dot(flat, up_all[expert], preferred_element_type=jnp.float32)
        hidden = (jax.nn.silu(gate) * upper).astype(jnp.bfloat16)
        summed = down_sum(hidden, down_all[expert])
        answers.append(summed.astype(jnp.bfloat16).reshape(sources, CAP, EMBED_DIMENSION))
    answer = jnp.stack(answers)
    picked = answer[pick, source, slot].astype(jnp.float32)
    return (wide + weight * picked).astype(jnp.bfloat16)

def reference(transit_activation, incoming_queue, expert_assignment, rescale_factor, routing_matrix, gating_matrix, expand_matrix, contract_matrix):
    present_carry = [transit_activation[advance_level] for advance_level in range(N_SECTION)]
    side = [incoming_queue[advance_level] for advance_level in range(N_SECTION)]
    for tick in range(TICKS):
        for layer in range(N_SECTION):
            place = (layer - tick) % N_SECTION
            present_carry[place] = layer_apply(present_carry[place], expert_assignment[layer, tick], rescale_factor[layer], routing_matrix[layer], gating_matrix[layer], expand_matrix[layer], contract_matrix[layer])
        arriving = -(tick + 1) % N_SECTION
        present_carry[arriving], side[arriving] = (side[arriving], present_carry[arriving])
    held = [present_carry[(j - TICKS) % N_SECTION] for j in range(N_SECTION)]
    waiting = [side[(j - TICKS) % N_SECTION] for j in range(N_SECTION)]
    return (jnp.stack(held), jnp.stack(waiting))
```

```python
import functools

import jax
import jax.numpy as jnp
from jax import lax
from jax.experimental import pallas as pl
from jax.experimental.pallas import tpu as pltpu
from jax.sharding import PartitionSpec as P

EPSILON = 1e-06
LANES = 128
MOST_ROTATIONS = 7


def relay(sections, ticks):
    current = [("transit", s) for s in range(sections)]
    side = [("incoming", s) for s in range(sections)]
    reads = {}
    for tick in range(ticks):
        for s in range(sections):
            reads[s, tick] = current[s]
        done = [("done", s, tick) for s in range(sections)]
        current = [side[-1]] + done[:-1]
        side = [done[-1]] + side[:-1]
    return reads, current, side


def waves_of(sections, ticks):
    reads, *_ = relay(sections, ticks)
    level = {}
    for s, tick in sorted(reads, key=lambda job: job[1]):
        source = reads[s, tick]
        level[s, tick] = level[source[1:]] + 1 if source[0] == "done" else 0
    depth = max(level.values()) + 1
    tail = {}
    for job in sorted(reads, key=lambda job: -job[1]):
        after = [tail[other] for other, source in reads.items() if source == ("done",) + job]
        tail[job] = 1 + max(after, default=0)
    for slots in range(1, ticks + 1):
        placed, waves = {}, []
        for wave in range(depth):
            row = []
            for s in range(sections):
                ready = [
                    job
                    for job in reads
                    if job[0] == s
                    and job not in placed
                    and (reads[job][0] != "done" or placed.get(reads[job][1:], wave) < wave)
                ]
                ready.sort(key=lambda job: (-tail[job], job[1]))
                row.append(ready[:slots])
            for jobs in row:
                placed.update({job: wave for job in jobs})
            waves.append([[jobs[i] if i < len(jobs) else None for jobs in row] for i in range(slots)])
        if len(placed) == len(reads):
            return waves
    raise ValueError("no plan")


class Store:
    def __init__(self, needs):
        self.needs = needs
        self.found = {}
        self.arrays = {}

    def add(self, key, array, tokens):
        self.arrays[key] = array
        perms = []
        for slot, row in enumerate(tokens):
            for s, value in enumerate(row):
                if value is None:
                    continue
                self.found[value, s] = (key, slot)
                for wanted, reader in sorted(self.needs):
                    if wanted != value or reader == s:
                        continue
                    for n, perm in enumerate(perms):
                        if perm.get(reader, s) == s and all(
                            a == reader for a, b in perm.items() if b == s
                        ):
                            break
                    else:
                        n, perm = len(perms), {}
                        perms.append(perm)
                    perm[reader] = s
                    self.found[value, reader] = ((key, n), slot)
        for n, perm in enumerate(perms):
            route = sorted((b, a) for a, b in perm.items())
            self.arrays[key, n] = lax.ppermute(array, "section", route)

    def read(self, row, section):
        options = {}
        for s, value in enumerate(row):
            if value is not None:
                options.setdefault(self.found[value, s], []).append(s)
        picked = None
        for (key, slot), readers in options.items():
            block = self.arrays[key][slot]
            if picked is None:
                picked = block
                continue
            here = functools.reduce(jnp.logical_or, [section == s for s in readers])
            picked = jnp.where(here, block, picked)
        return picked


def rotated(block, axis, distance):
    size = lax.axis_size(axis)
    return lax.ppermute(block, axis, [(i, (i + distance) % size) for i in range(size)])


def spread(block, axis):
    size = lax.axis_size(axis)
    if size - 1 > MOST_ROTATIONS:
        copies = jnp.broadcast_to(block[None], (size,) + block.shape)
        got = lax.all_to_all(copies, axis, 0, 0, tiled=True)
        return [got[i] for i in range(size)]
    return [block] + [rotated(block, axis, k) for k in range(1, size)]


def collect(chunks, axis):
    size = lax.axis_size(axis)
    if size - 1 > MOST_ROTATIONS:
        got = lax.all_to_all(jnp.stack(chunks), axis, 0, 0, tiled=True)
        return [got[i] for i in range(size)]
    return [chunks[0]] + [rotated(chunks[k], axis, -k) for k in range(1, size)]


def expert_kernel(pieces, tile_hidden, tile_out, *refs):
    chunks = refs[:pieces]
    gain_ref, table_ref, gate_ref, up_ref, down_ref = refs[pieces : pieces + 5]
    outs = refs[pieces + 5 : -3]
    rows_ref, normed_ref, hidden_ref = refs[-3:]
    width = gain_ref.shape[1]
    hidden_units = gate_ref.shape[1]
    start = 0
    for chunk in chunks:
        count = chunk.shape[0]
        rows_ref[start : start + count, :] = chunk[...].astype(jnp.float32)
        start += count
    rows = rows_ref[:, :width]
    pick = rows_ref[:, width : width + 1]
    square = jnp.mean(rows * rows, axis=-1, keepdims=True)
    normed = (rows * lax.rsqrt(square + EPSILON) * gain_ref[...]).astype(jnp.bfloat16)
    normed_ref[...] = normed
    wide = normed.astype(jnp.float32)
    table = table_ref[...].astype(jnp.float32)
    first = jnp.sum(wide * table[0:1], axis=-1, keepdims=True)
    second = jnp.sum(wide * table[1:2], axis=-1, keepdims=True)
    margin = jnp.where(pick < 0.5, first - second, second - first)
    weight = 1.0 / (1.0 + jnp.exp(-margin))
    mine = lax.axis_index("pair").astype(jnp.float32)
    chosen = jnp.broadcast_to(jnp.abs(pick - mine) < 0.5, (start, tile_out))

    def hidden_step(step, carry):
        at = pl.ds(pl.multiple_of(step * tile_hidden, tile_hidden), tile_hidden)
        gate = jnp.dot(normed_ref[...], gate_ref[:, at], preferred_element_type=jnp.float32)
        upper = jnp.dot(normed_ref[...], up_ref[:, at], preferred_element_type=jnp.float32)
        hidden_ref[:, at] = (gate / (1.0 + jnp.exp(-gate)) * upper).astype(jnp.bfloat16)
        return carry

    lax.fori_loop(0, hidden_units // tile_hidden, hidden_step, None)

    def out_step(step, carry):
        at = pl.ds(pl.multiple_of(step * tile_out, tile_out), tile_out)
        part = jnp.dot(hidden_ref[...], down_ref[:, at], preferred_element_type=jnp.float32)
        part = jnp.where(chosen, part * weight, 0.0).astype(jnp.bfloat16)
        share = start // len(outs)
        for n, out in enumerate(outs):
            out[:, at] = part[n * share : (n + 1) * share]
        return carry

    lax.fori_loop(0, width // tile_out, out_step, None)


def tile_of(size, most):
    tile = most
    while size % tile:
        tile //= 2
    return tile


def expert_call(chunks, gain, table, gate_w, up_w, down_w, parts):
    width, hidden_units = gate_w.shape
    rows = sum(chunk.shape[0] for chunk in chunks)
    whole = pl.BlockSpec(memory_space=pltpu.VMEM)
    weights = gate_w.size + up_w.size + down_w.size
    return pl.pallas_call(
        functools.partial(
            expert_kernel, len(chunks), tile_of(hidden_units, 1024), tile_of(width, 1024)
        ),
        out_shape=[jax.ShapeDtypeStruct((rows // parts, width), jnp.bfloat16)] * parts,
        in_specs=[whole] * (len(chunks) + 5),
        out_specs=[whole] * parts,
        scratch_shapes=[
            pltpu.VMEM((rows, width + LANES), jnp.float32),
            pltpu.VMEM((rows, width), jnp.bfloat16),
            pltpu.VMEM((rows, hidden_units), jnp.bfloat16),
        ],
        compiler_params=pltpu.CompilerParams(vmem_limit_bytes=20 << 20),
        cost_estimate=pl.CostEstimate(
            flops=2 * rows * weights, bytes_accessed=2 * weights, transcendentals=rows * hidden_units
        ),
    )(*chunks, gain, table, gate_w, up_w, down_w)


def layer(rows, picks, gain, table, weights):
    count, width = rows.shape
    mark = jnp.broadcast_to(picks.astype(rows.dtype)[:, None], (count, LANES))
    packed = jnp.concatenate([rows, mark], axis=1)
    near = spread(packed, "expert")
    by_core = [spread(block, "pair") for block in near]
    cores = lax.axis_size("pair")
    chunks = [by_core[k][q] for q in range(cores) for k in range(len(near))]
    parts = expert_call(chunks, gain, table, *weights, cores)
    met = collect(parts, "pair")
    total = functools.reduce(jnp.add, met)
    shares = [total[k * count : (k + 1) * count] for k in range(len(near))]
    got = collect(shares, "expert")
    answer = functools.reduce(jnp.add, [piece.astype(jnp.float32) for piece in got])
    return (rows.astype(jnp.float32) + answer).astype(rows.dtype)


def body(
    transit_activation,
    incoming_queue,
    expert_assignment,
    rescale_factor,
    routing_matrix,
    gating_matrix,
    expand_matrix,
    contract_matrix,
):
    sections = lax.axis_size("section")
    section = lax.axis_index("section")
    ticks, tokens = expert_assignment.shape[1:3]
    width = transit_activation.shape[-1]
    table = routing_matrix[0].T
    weights = [
        pltpu.with_memory_space_constraint(w[0, 0], pltpu.VMEM)
        for w in (gating_matrix, expand_matrix, contract_matrix)
    ]
    reads, last, left = relay(sections, ticks)
    waves = waves_of(sections, ticks)
    needs = {(source, job[0]) for job, source in reads.items()}
    needs |= {(value, s) for s, value in enumerate(last)}
    needs |= {(value, s) for s, value in enumerate(left)}
    store = Store(needs)
    store.add("incoming", incoming_queue, [[("incoming", s) for s in range(sections)]])
    store.add("transit", transit_activation, [[("transit", s) for s in range(sections)]])
    for number, wave in enumerate(waves):
        rows, picks = [], []
        for row in wave:
            rows.append(store.read([job and reads[job] for job in row], section))
            at = [job[1] for job in row if job]
            which = jnp.int32(at[0])
            for s, job in enumerate(row):
                if job and job[1] != at[0]:
                    which = jnp.where(section == s, job[1], which)
            if len(set(at)) == 1:
                picks.append(expert_assignment[0, at[0], :, 0])
            else:
                picks.append(lax.dynamic_index_in_dim(expert_assignment[0, :, :, 0], which, 0, False))
        out = layer(
            jnp.concatenate(rows, axis=0), jnp.concatenate(picks, axis=0), rescale_factor, table, weights
        )
        tokens_of = [[job and ("done",) + job for job in row] for row in wave]
        store.add(number, out.reshape(len(wave), tokens, width), tokens_of)
    return (
        store.read(last, section)[None],
        store.read(left, section)[None],
    )


def solution(mesh):
    in_specs = (
        P("section", ("groups", "expert", "pair"), None),
        P("section", ("groups", "expert", "pair"), None),
        P("section", None, ("groups", "expert", "pair"), None),
        P("section", None),
        P("section", None, None),
        P("section", "pair", None, "expert"),
        P("section", "pair", None, "expert"),
        P("section", "pair", "expert", None),
    )
    out_specs = (
        P("section", ("groups", "expert", "pair"), None),
        P("section", ("groups", "expert", "pair"), None),
    )
    return jax.shard_map(body, mesh=mesh, in_specs=in_specs, out_specs=out_specs, check_vma=False)
```

```python
import functools

import jax
import jax.numpy as jnp
from jax import lax
from jax.experimental import pallas as pl
from jax.experimental.pallas import tpu as pltpu
from jax.sharding import PartitionSpec as P

EPSILON = 1e-06
LANES = 128
MOST_ROTATIONS = 7


def relay(sections, ticks):
    current = [("transit", s) for s in range(sections)]
    side = [("incoming", s) for s in range(sections)]
    reads = {}
    for tick in range(ticks):
        for s in range(sections):
            reads[s, tick] = current[s]
        done = [("done", s, tick) for s in range(sections)]
        current = [side[-1]] + done[:-1]
        side = [done[-1]] + side[:-1]
    return reads, current, side


def waves_of(sections, ticks):
    reads, *_ = relay(sections, ticks)
    level = {}
    for s, tick in sorted(reads, key=lambda job: job[1]):
        source = reads[s, tick]
        level[s, tick] = level[source[1:]] + 1 if source[0] == "done" else 0
    depth = max(level.values()) + 1
    tail = {}
    for job in sorted(reads, key=lambda job: -job[1]):
        after = [tail[other] for other, source in reads.items() if source == ("done",) + job]
        tail[job] = 1 + max(after, default=0)
    for slots in range(1, ticks + 1):
        placed, waves = {}, []
        for wave in range(depth):
            row = []
            for s in range(sections):
                ready = [
                    job
                    for job in reads
                    if job[0] == s
                    and job not in placed
                    and (reads[job][0] != "done" or placed.get(reads[job][1:], wave) < wave)
                ]
                ready.sort(key=lambda job: (-tail[job], job[1]))
                row.append(ready[:slots])
            for jobs in row:
                placed.update({job: wave for job in jobs})
            waves.append([[jobs[i] if i < len(jobs) else None for jobs in row] for i in range(slots)])
        if len(placed) == len(reads):
            return waves
    raise ValueError("no plan")


class Store:
    def __init__(self, needs, tokens):
        self.needs = needs
        self.tokens = tokens
        self.found = {}
        self.arrays = {}

    def add(self, key, array, held):
        self.arrays[key] = array
        perms = []
        for slot, row in enumerate(held):
            for s, value in enumerate(row):
                if value is None:
                    continue
                self.found[value, s] = (key, slot)
                for wanted, reader in sorted(self.needs):
                    if wanted != value or reader == s:
                        continue
                    for n, perm in enumerate(perms):
                        if perm.get(reader, s) == s and all(
                            a == reader for a, b in perm.items() if b == s
                        ):
                            break
                    else:
                        n, perm = len(perms), {}
                        perms.append(perm)
                    perm[reader] = s
                    self.found[value, reader] = ((key, n), slot)
        for n, perm in enumerate(perms):
            route = sorted((b, a) for a, b in perm.items())
            self.arrays[key, n] = lax.ppermute(array, "section", route)

    def choices(self, wanted):
        keys, table = [], []
        for row in wanted:
            options = {}
            for s, value in enumerate(row):
                if value is None:
                    continue
                key, slot = self.found[value, s]
                if key not in keys:
                    keys.append(key)
                options.setdefault((keys.index(key), slot * self.tokens), []).append(s)
            table.append(list(options.items()))
        return [self.arrays[key] for key in keys], table


WHOLE = pl.BlockSpec(memory_space=pltpu.VMEM)


def near(array):
    return pltpu.with_memory_space_constraint(array, pltpu.VMEM)


def small_limit():
    return pltpu.CompilerParams(vmem_limit_bytes=8 << 20)


def by_section(options, value_of):
    section = lax.axis_index("section")
    picked = value_of(options[0][0])
    for option, readers in options[1:]:
        here = functools.reduce(jnp.logical_or, [section == s for s in readers])
        picked = jnp.where(here, value_of(option), picked)
    return picked


def pack_kernel(table, ticks, tokens, count, *refs):
    arrays, assign_ref, packed_ref, wide_ref = refs[:count], *refs[count:]
    width = packed_ref.shape[1] - LANES
    lane = lax.broadcasted_iota(jnp.int32, (tokens, LANES), 0)
    for slot, options in enumerate(table):
        at = slice(slot * tokens, (slot + 1) * tokens)
        wide_ref[at, :width] = by_section(
            options, lambda where: arrays[where[0]][where[1] : where[1] + tokens, :].astype(jnp.float32)
        )
        mark = jnp.zeros((tokens, LANES), jnp.int32)
        for row in range(tokens):
            pick = by_section(ticks[slot], lambda tick: assign_ref[row, tick])
            mark = jnp.where(lane == row, pick, mark)
        wide_ref[at, width:] = mark.astype(jnp.float32)
    packed_ref[...] = wide_ref[...].astype(packed_ref.dtype)


def pack(arrays, table, ticks, assign, tokens):
    rows, width = len(table) * tokens, arrays[0].shape[1] + LANES
    return pl.pallas_call(
        functools.partial(pack_kernel, table, ticks, tokens, len(arrays)),
        out_shape=pltpu.VMEM((rows, width), arrays[0].dtype),
        in_specs=[WHOLE] * len(arrays) + [pl.BlockSpec(memory_space=pltpu.SMEM)],
        out_specs=WHOLE,
        scratch_shapes=[pltpu.VMEM((rows, width), jnp.float32)],
        compiler_params=small_limit(),
    )(*[near(array) for array in arrays], assign)


def pick_kernel(tables, tokens, count, *refs):
    for table, out in zip(tables, refs[count:]):
        out[0] = by_section(table[0], lambda where: refs[where[0]][where[1] : where[1] + tokens, :])


def pick_out(arrays, tables, tokens):
    shape = (1, tokens, arrays[0].shape[1])
    return pl.pallas_call(
        functools.partial(pick_kernel, tables, tokens, len(arrays)),
        out_shape=[jax.ShapeDtypeStruct(shape, arrays[0].dtype)] * len(tables),
        in_specs=[WHOLE] * len(arrays),
        out_specs=[WHOLE] * len(tables),
        compiler_params=small_limit(),
    )(*[near(array) for array in arrays])


def meet_kernel(count, *refs):
    parts, outs, total_ref = refs[:count], refs[count:-1], refs[-1]
    total_ref[...] = functools.reduce(jnp.add, [part[...].astype(jnp.float32) for part in parts])
    share = outs[0].shape[0]
    for k, out in enumerate(outs):
        out[...] = total_ref[k * share : (k + 1) * share, :].astype(out.dtype)


def meet(parts, shares):
    rows, width = parts[0].shape
    return pl.pallas_call(
        functools.partial(meet_kernel, len(parts)),
        out_shape=[pltpu.VMEM((rows // shares, width), parts[0].dtype)] * shares,
        in_specs=[WHOLE] * len(parts),
        out_specs=[WHOLE] * shares,
        scratch_shapes=[pltpu.VMEM((rows, width), jnp.float32)],
        compiler_params=small_limit(),
    )(*[near(part) for part in parts])


def add_kernel(packed_ref, *refs):
    pieces, out = refs[:-1], refs[-1]
    width = out.shape[1]
    total = functools.reduce(jnp.add, [piece[...].astype(jnp.float32) for piece in pieces])
    out[...] = (packed_ref[:, :width].astype(jnp.float32) + total).astype(out.dtype)


def add_rows(packed, pieces):
    return pl.pallas_call(
        add_kernel,
        out_shape=pltpu.VMEM(pieces[0].shape, packed.dtype),
        in_specs=[WHOLE] * (1 + len(pieces)),
        out_specs=WHOLE,
        compiler_params=small_limit(),
    )(near(packed), *[near(piece) for piece in pieces])


def partner(block, axis, distance, back=False):
    size = lax.axis_size(axis)
    if size & (size - 1) == 0:
        return lax.ppermute(block, axis, [(i, i ^ distance) for i in range(size)])
    step = -distance if back else distance
    return lax.ppermute(block, axis, [(i, (i + step) % size) for i in range(size)])


def wide_axis(axis):
    return lax.axis_size(axis) - 1 > MOST_ROTATIONS


def spread(block, axis):
    size = lax.axis_size(axis)
    if wide_axis(axis):
        copies = jnp.broadcast_to(block[None], (size,) + block.shape)
        got = lax.all_to_all(copies, axis, 0, 0, tiled=True)
        return [got.reshape(size * block.shape[0], block.shape[1])]
    return [block] + [partner(block, axis, k) for k in range(1, size)]


def collect(chunks, axis):
    size = lax.axis_size(axis)
    if wide_axis(axis):
        got = lax.all_to_all(jnp.stack(chunks), axis, 0, 0, tiled=True)
        return [got[i] for i in range(size)]
    return [chunks[0]] + [partner(chunks[k], axis, k, True) for k in range(1, size)]


def expert_kernel(pieces, cores, loads, tiles, *refs):
    chunks = refs[:pieces]
    gain_ref, table_ref = refs[pieces : pieces + 2]
    given = refs[pieces + 2 : pieces + 5]
    outs = refs[pieces + 5 : pieces + 5 + cores]
    scratch = refs[pieces + 5 + cores :]
    copies = None
    if loads:
        held, scratch = scratch[:3], scratch[3:]
        scratch, sems = scratch[:-1], scratch[-1]
        copies = []
        for tile in range(tiles):
            for n in (0, 1):
                copies.append((n, tile))
        copies += [(2, tile) for tile in range(tiles)]

        def copy_of(n, tile):
            size = held[n].shape[1] // tiles
            at = pl.ds(tile * size, size)
            return pltpu.make_async_copy(given[n].at[:, at], held[n].at[:, at], sems.at[n, tile])

        for n, tile in copies:
            copy_of(n, tile).start()
    else:
        held = given
    gate_ref, up_ref, down_ref = held
    rows_ref, normed_ref, hidden_ref = scratch
    width = gain_ref.shape[1]
    start = 0
    for chunk in chunks:
        count = chunk.shape[0]
        rows_ref[start : start + count, :] = chunk[...].astype(jnp.float32)
        start += count
    rows = rows_ref[:, :width]
    pick = rows_ref[:, width : width + 1]
    square = jnp.mean(rows * rows, axis=-1, keepdims=True)
    normed = (rows * lax.rsqrt(square + EPSILON) * gain_ref[...]).astype(jnp.bfloat16)
    normed_ref[...] = normed
    wide = normed.astype(jnp.float32)
    table = table_ref[...].astype(jnp.float32)
    first = jnp.sum(wide * table[0:1], axis=-1, keepdims=True)
    second = jnp.sum(wide * table[1:2], axis=-1, keepdims=True)
    margin = jnp.where(pick < 0.5, first - second, second - first)
    weight = 1.0 / (1.0 + jnp.exp(-margin))
    mine = lax.axis_index("pair").astype(jnp.float32)
    for tile in range(tiles):
        size = gate_ref.shape[1] // tiles
        at = slice(tile * size, (tile + 1) * size)
        if loads:
            copy_of(0, tile).wait()
        gate = jnp.dot(normed_ref[...], gate_ref[:, at], preferred_element_type=jnp.float32)
        if loads:
            copy_of(1, tile).wait()
        upper = jnp.dot(normed_ref[...], up_ref[:, at], preferred_element_type=jnp.float32)
        hidden_ref[:, at] = (gate / (1.0 + jnp.exp(-gate)) * upper).astype(jnp.bfloat16)
    for tile in range(tiles):
        size = width // tiles
        at = slice(tile * size, (tile + 1) * size)
        if loads:
            copy_of(2, tile).wait()
        part = jnp.dot(hidden_ref[...], down_ref[:, at], preferred_element_type=jnp.float32)
        chosen = jnp.broadcast_to(jnp.abs(pick - mine) < 0.5, part.shape)
        part = jnp.where(chosen, part * weight, 0.0).astype(jnp.bfloat16)
        share = start // cores
        for n, out in enumerate(outs):
            out[:, at] = part[n * share : (n + 1) * share]


def tiles_of(width, hidden_units):
    tiles = 4
    while width % (tiles * LANES) or hidden_units % (tiles * LANES):
        tiles //= 2
    return tiles


def expert_call(chunks, gain, table, weights, cores, loads):
    width, hidden_units = weights[0].shape
    rows = sum(chunk.shape[0] for chunk in chunks)
    count = sum(w.size for w in weights)
    tiles = tiles_of(width, hidden_units)
    out_shape = [pltpu.VMEM((rows // cores, width), jnp.bfloat16)] * cores
    scratch = [
        pltpu.VMEM((rows, width + LANES), jnp.float32),
        pltpu.VMEM((rows, width), jnp.bfloat16),
        pltpu.VMEM((rows, hidden_units), jnp.bfloat16),
    ]
    if loads:
        out_shape += [pltpu.VMEM(w.shape, w.dtype) for w in weights]
        scratch.append(pltpu.SemaphoreType.DMA((3, tiles)))
        weights = [pltpu.with_memory_space_constraint(w, pltpu.HBM) for w in weights]
    else:
        weights = [near(w) for w in weights]
    result = pl.pallas_call(
        functools.partial(expert_kernel, len(chunks), cores, loads, tiles),
        out_shape=out_shape,
        in_specs=[WHOLE] * (len(chunks) + 2)
        + [pl.BlockSpec(memory_space=pltpu.HBM) if loads else WHOLE] * 3,
        out_specs=[WHOLE] * len(out_shape),
        scratch_shapes=scratch,
        compiler_params=pltpu.CompilerParams(vmem_limit_bytes=12 << 20),
        cost_estimate=pl.CostEstimate(
            flops=2 * rows * count, bytes_accessed=2 * count, transcendentals=rows * hidden_units
        ),
    )(*[near(chunk) for chunk in chunks], near(gain), near(table), *weights)
    return result[:cores], result[cores:]


def layer(packed, gain, table, weights, loads):
    far = spread(packed, "expert")
    by_core = [spread(block, "pair") for block in far]
    cores, shares = lax.axis_size("pair"), lax.axis_size("expert")
    chunks = [by_core[k][q] for q in range(cores) for k in range(len(far))]
    parts, held = expert_call(chunks, gain, table, weights, cores, loads)
    shares = meet(collect(parts, "pair"), shares)
    return add_rows(packed, collect(shares, "expert")), held or weights


def body(
    transit_activation,
    incoming_queue,
    expert_assignment,
    rescale_factor,
    routing_matrix,
    gating_matrix,
    expand_matrix,
    contract_matrix,
):
    sections = lax.axis_size("section")
    ticks, tokens = expert_assignment.shape[1:3]
    table = routing_matrix[0].T
    assign = expert_assignment[0, :, :, 0].T
    weights = [w[0, 0] for w in (gating_matrix, expand_matrix, contract_matrix)]
    reads, last, left = relay(sections, ticks)
    needs = {(source, job[0]) for job, source in reads.items()}
    needs |= {(value, s) for s, value in enumerate(last)}
    needs |= {(value, s) for s, value in enumerate(left)}
    store = Store(needs, tokens)
    store.add("incoming", incoming_queue[0], [[("incoming", s) for s in range(sections)]])
    store.add("transit", transit_activation[0], [[("transit", s) for s in range(sections)]])
    for number, wave in enumerate(waves_of(sections, ticks)):
        arrays, where = store.choices([[job and reads[job] for job in row] for row in wave])
        when = []
        for row in wave:
            options = {}
            for s, job in enumerate(row):
                if job:
                    options.setdefault(job[1], []).append(s)
            when.append(list(options.items()))
        packed = pack(arrays, where, when, assign, tokens)
        out, weights = layer(packed, rescale_factor, table, weights, number == 0)
        store.add(number, out, [[job and ("done",) + job for job in row] for row in wave])
    arrays, where = store.choices([last, left])
    return pick_out(arrays, [[options] for options in where], tokens)


def solution(mesh):
    in_specs = (
        P("section", ("groups", "expert", "pair"), None),
        P("section", ("groups", "expert", "pair"), None),
        P("section", None, ("groups", "expert", "pair"), None),
        P("section", None),
        P("section", None, None),
        P("section", "pair", None, "expert"),
        P("section", "pair", None, "expert"),
        P("section", "pair", "expert", None),
    )
    out_specs = (
        P("section", ("groups", "expert", "pair"), None),
        P("section", ("groups", "expert", "pair"), None),
    )
    return jax.shard_map(body, mesh=mesh, in_specs=in_specs, out_specs=out_specs, check_vma=False)
```

```python
import functools

import jax
import jax.numpy as jnp
from jax import lax
from jax.experimental import pallas as pl
from jax.experimental.pallas import tpu as pltpu
from jax.sharding import PartitionSpec as P

EPSILON = 1e-06
LANES = 128
MOST_ROTATIONS = 7


def relay(sections, ticks):
    current = [("transit", s) for s in range(sections)]
    side = [("incoming", s) for s in range(sections)]
    reads = {}
    for tick in range(ticks):
        for s in range(sections):
            reads[s, tick] = current[s]
        done = [("done", s, tick) for s in range(sections)]
        current = [side[-1]] + done[:-1]
        side = [done[-1]] + side[:-1]
    return reads, current, side


def waves_of(sections, ticks):
    reads, *_ = relay(sections, ticks)
    level = {}
    for s, tick in sorted(reads, key=lambda job: job[1]):
        source = reads[s, tick]
        level[s, tick] = level[source[1:]] + 1 if source[0] == "done" else 0
    depth = max(level.values()) + 1
    tail = {}
    for job in sorted(reads, key=lambda job: -job[1]):
        after = [tail[other] for other, source in reads.items() if source == ("done",) + job]
        tail[job] = 1 + max(after, default=0)
    for slots in range(1, ticks + 1):
        placed, waves = {}, []
        for wave in range(depth):
            row = []
            for s in range(sections):
                ready = [
                    job
                    for job in reads
                    if job[0] == s
                    and job not in placed
                    and (reads[job][0] != "done" or placed.get(reads[job][1:], wave) < wave)
                ]
                ready.sort(key=lambda job: (-tail[job], job[1]))
                row.append(ready[:slots])
            for jobs in row:
                placed.update({job: wave for job in jobs})
            waves.append([[jobs[i] if i < len(jobs) else None for jobs in row] for i in range(slots)])
        if len(placed) == len(reads):
            return waves
    raise ValueError("no plan")


class Store:
    def __init__(self, needs, tokens):
        self.needs = needs
        self.tokens = tokens
        self.found = {}
        self.arrays = {}

    def add(self, key, array, held):
        self.arrays[key] = array
        perms = []
        for slot, row in enumerate(held):
            for s, value in enumerate(row):
                if value is None:
                    continue
                self.found[value, s] = (key, slot)
                for wanted, reader in sorted(self.needs):
                    if wanted != value or reader == s:
                        continue
                    for n, perm in enumerate(perms):
                        if perm.get(reader, s) == s and all(
                            a == reader for a, b in perm.items() if b == s
                        ):
                            break
                    else:
                        n, perm = len(perms), {}
                        perms.append(perm)
                    perm[reader] = s
                    self.found[value, reader] = ((key, n), slot)
        for n, perm in enumerate(perms):
            route = sorted((b, a) for a, b in perm.items())
            self.arrays[key, n] = lax.ppermute(array, "section", route)

    def choices(self, wanted):
        keys, table = [], []
        for row in wanted:
            options = {}
            for s, value in enumerate(row):
                if value is None:
                    continue
                key, slot = self.found[value, s]
                if key not in keys:
                    keys.append(key)
                options.setdefault((keys.index(key), slot * self.tokens), []).append(s)
            table.append(list(options.items()))
        return [self.arrays[key] for key in keys], table


WHOLE = pl.BlockSpec(memory_space=pltpu.VMEM)


def near(array):
    return pltpu.with_memory_space_constraint(array, pltpu.VMEM)


def small_limit():
    return pltpu.CompilerParams(vmem_limit_bytes=8 << 20)


def by_section(options, value_of):
    section = lax.axis_index("section")
    picked = value_of(options[0][0])
    for option, readers in options[1:]:
        here = functools.reduce(jnp.logical_or, [section == s for s in readers])
        picked = jnp.where(here, value_of(option), picked)
    return picked


def pack_kernel(table, ticks, tokens, count, *refs):
    arrays, assign_ref, packed_ref, wide_ref = refs[:count], *refs[count:]
    width = packed_ref.shape[1] - LANES
    lane = lax.broadcasted_iota(jnp.int32, (tokens, LANES), 0)
    for slot, options in enumerate(table):
        at = slice(slot * tokens, (slot + 1) * tokens)
        wide_ref[at, :width] = by_section(
            options, lambda where: arrays[where[0]][where[1] : where[1] + tokens, :].astype(jnp.float32)
        )
        mark = jnp.zeros((tokens, LANES), jnp.int32)
        for row in range(tokens):
            pick = by_section(ticks[slot], lambda tick: assign_ref[row, tick])
            mark = jnp.where(lane == row, pick, mark)
        wide_ref[at, width:] = mark.astype(jnp.float32)
    packed_ref[...] = wide_ref[...].astype(packed_ref.dtype)


def pack(arrays, table, ticks, assign, tokens):
    rows, width = len(table) * tokens, arrays[0].shape[1] + LANES
    return pl.pallas_call(
        functools.partial(pack_kernel, table, ticks, tokens, len(arrays)),
        out_shape=pltpu.VMEM((rows, width), arrays[0].dtype),
        in_specs=[WHOLE] * len(arrays) + [pl.BlockSpec(memory_space=pltpu.SMEM)],
        out_specs=WHOLE,
        scratch_shapes=[pltpu.VMEM((rows, width), jnp.float32)],
        compiler_params=small_limit(),
    )(*[near(array) for array in arrays], assign)


def pick_kernel(tables, tokens, count, *refs):
    for table, out in zip(tables, refs[count:]):
        out[0] = by_section(table[0], lambda where: refs[where[0]][where[1] : where[1] + tokens, :])


def pick_out(arrays, tables, tokens):
    shape = (1, tokens, arrays[0].shape[1])
    return pl.pallas_call(
        functools.partial(pick_kernel, tables, tokens, len(arrays)),
        out_shape=[jax.ShapeDtypeStruct(shape, arrays[0].dtype)] * len(tables),
        in_specs=[WHOLE] * len(arrays),
        out_specs=[WHOLE] * len(tables),
        compiler_params=small_limit(),
    )(*[near(array) for array in arrays])


def meet_kernel(count, *refs):
    parts, outs, total_ref = refs[:count], refs[count:-1], refs[-1]
    total_ref[...] = functools.reduce(jnp.add, [part[...].astype(jnp.float32) for part in parts])
    share = outs[0].shape[0]
    for k, out in enumerate(outs):
        out[...] = total_ref[k * share : (k + 1) * share, :].astype(out.dtype)


def meet(parts, shares):
    rows, width = parts[0].shape
    return pl.pallas_call(
        functools.partial(meet_kernel, len(parts)),
        out_shape=[pltpu.VMEM((rows // shares, width), parts[0].dtype)] * shares,
        in_specs=[WHOLE] * len(parts),
        out_specs=[WHOLE] * shares,
        scratch_shapes=[pltpu.VMEM((rows, width), jnp.float32)],
        compiler_params=small_limit(),
    )(*[near(part) for part in parts])


def add_kernel(packed_ref, *refs):
    pieces, out = refs[:-1], refs[-1]
    width = out.shape[1]
    total = functools.reduce(jnp.add, [piece[...].astype(jnp.float32) for piece in pieces])
    out[...] = (packed_ref[:, :width].astype(jnp.float32) + total).astype(out.dtype)


def add_rows(packed, pieces):
    return pl.pallas_call(
        add_kernel,
        out_shape=pltpu.VMEM(pieces[0].shape, packed.dtype),
        in_specs=[WHOLE] * (1 + len(pieces)),
        out_specs=WHOLE,
        compiler_params=small_limit(),
    )(near(packed), *[near(piece) for piece in pieces])


def partner(block, axis, distance, back=False):
    size = lax.axis_size(axis)
    if size & (size - 1) == 0:
        return lax.ppermute(block, axis, [(i, i ^ distance) for i in range(size)])
    step = -distance if back else distance
    return lax.ppermute(block, axis, [(i, (i + step) % size) for i in range(size)])


def wide_axis(axis):
    return lax.axis_size(axis) - 1 > MOST_ROTATIONS


def spread(block, axis):
    size = lax.axis_size(axis)
    if wide_axis(axis):
        copies = jnp.broadcast_to(block[None], (size,) + block.shape)
        got = lax.all_to_all(copies, axis, 0, 0, tiled=True)
        return [got.reshape(size * block.shape[0], block.shape[1])]
    return [block] + [partner(block, axis, k) for k in range(1, size)]


def collect(chunks, axis):
    size = lax.axis_size(axis)
    if wide_axis(axis):
        got = lax.all_to_all(jnp.stack(chunks), axis, 0, 0, tiled=True)
        return [got[i] for i in range(size)]
    return [chunks[0]] + [partner(chunks[k], axis, k, True) for k in range(1, size)]


def expert_kernel(pieces, cores, loads, tiles, *refs):
    chunks = refs[:pieces]
    gain_ref, table_ref = refs[pieces : pieces + 2]
    given = refs[pieces + 2 : pieces + 5]
    outs = refs[pieces + 5 : pieces + 5 + cores]
    scratch = refs[pieces + 5 + cores :]
    copies = None
    if loads:
        held, scratch = scratch[:3], scratch[3:]
        scratch, sems = scratch[:-1], scratch[-1]
        copies = []
        for tile in range(tiles):
            for n in (0, 1):
                copies.append((n, tile))
        copies += [(2, tile) for tile in range(tiles)]

        def copy_of(n, tile):
            size = held[n].shape[1] // tiles
            at = pl.ds(tile * size, size)
            return pltpu.make_async_copy(given[n].at[:, at], held[n].at[:, at], sems.at[n, tile])

        for n, tile in copies:
            copy_of(n, tile).start()
    else:
        held = given
    gate_ref, up_ref, down_ref = held
    rows_ref, normed_ref, hidden_ref = scratch
    width = gain_ref.shape[1]
    start = 0
    for chunk in chunks:
        count = chunk.shape[0]
        rows_ref[start : start + count, :] = chunk[...].astype(jnp.float32)
        start += count
    rows = rows_ref[:, :width]
    pick = rows_ref[:, width : width + 1]
    square = jnp.mean(rows * rows, axis=-1, keepdims=True)
    normed = (rows * lax.rsqrt(square + EPSILON) * gain_ref[...]).astype(jnp.bfloat16)
    normed_ref[...] = normed
    wide = normed.astype(jnp.float32)
    table = table_ref[...].astype(jnp.float32)
    first = jnp.sum(wide * table[0:1], axis=-1, keepdims=True)
    second = jnp.sum(wide * table[1:2], axis=-1, keepdims=True)
    margin = jnp.where(pick < 0.5, first - second, second - first)
    weight = 1.0 / (1.0 + jnp.exp(-margin))
    mine = lax.axis_index("pair").astype(jnp.float32)
    for tile in range(tiles):
        size = gate_ref.shape[1] // tiles
        at = slice(tile * size, (tile + 1) * size)
        if loads:
            copy_of(0, tile).wait()
        gate = jnp.dot(normed_ref[...], gate_ref[:, at], preferred_element_type=jnp.float32)
        if loads:
            copy_of(1, tile).wait()
        upper = jnp.dot(normed_ref[...], up_ref[:, at], preferred_element_type=jnp.float32)
        hidden_ref[:, at] = (gate / (1.0 + jnp.exp(-gate)) * upper).astype(jnp.bfloat16)
    for tile in range(tiles):
        size = width // tiles
        at = slice(tile * size, (tile + 1) * size)
        if loads:
            copy_of(2, tile).wait()
        part = jnp.dot(hidden_ref[...], down_ref[:, at], preferred_element_type=jnp.float32)
        chosen = jnp.broadcast_to(jnp.abs(pick - mine) < 0.5, part.shape)
        part = jnp.where(chosen, part * weight, 0.0).astype(jnp.bfloat16)
        share = start // cores
        for n, out in enumerate(outs):
            out[:, at] = part[n * share : (n + 1) * share]


def tiles_of(width, hidden_units):
    tiles = 4
    while width % (tiles * LANES) or hidden_units % (tiles * LANES):
        tiles //= 2
    return tiles


def expert_call(chunks, gain, table, weights, cores, loads):
    width, hidden_units = weights[0].shape
    rows = sum(chunk.shape[0] for chunk in chunks)
    count = sum(w.size for w in weights)
    tiles = tiles_of(width, hidden_units)
    out_shape = [pltpu.VMEM((rows // cores, width), jnp.bfloat16)] * cores
    scratch = [
        pltpu.VMEM((rows, width + LANES), jnp.float32),
        pltpu.VMEM((rows, width), jnp.bfloat16),
        pltpu.VMEM((rows, hidden_units), jnp.bfloat16),
    ]
    if loads:
        out_shape += [pltpu.VMEM(w.shape, w.dtype) for w in weights]
        scratch.append(pltpu.SemaphoreType.DMA((3, tiles)))
        weights = [pltpu.with_memory_space_constraint(w, pltpu.HBM) for w in weights]
    else:
        weights = [near(w) for w in weights]
    result = pl.pallas_call(
        functools.partial(expert_kernel, len(chunks), cores, loads, tiles),
        out_shape=out_shape,
        in_specs=[WHOLE] * (len(chunks) + 2)
        + [pl.BlockSpec(memory_space=pltpu.HBM) if loads else WHOLE] * 3,
        out_specs=[WHOLE] * len(out_shape),
        scratch_shapes=scratch,
        compiler_params=pltpu.CompilerParams(vmem_limit_bytes=12 << 20),
        cost_estimate=pl.CostEstimate(
            flops=2 * rows * count, bytes_accessed=2 * count, transcendentals=rows * hidden_units
        ),
    )(*[near(chunk) for chunk in chunks], near(gain), near(table), *weights)
    return result[:cores], result[cores:]


def layer(packed, gain, table, weights, loads):
    far = spread(packed, "expert")
    by_core = [spread(block, "pair") for block in far]
    cores, shares = lax.axis_size("pair"), lax.axis_size("expert")
    chunks = [by_core[k][q] for q in range(cores) for k in range(len(far))]
    parts, held = expert_call(chunks, gain, table, weights, cores, loads)
    shares = meet(collect(parts, "pair"), shares)
    return add_rows(packed, collect(shares, "expert")), held or weights


SHORT = {
    (0, 0): (0, 0),
    (0, 1): (1, None),
    (1, 0): (None, 1),
    (1, 1): (2, 2),
}
NOBODY = -1
HBM = pl.BlockSpec(memory_space=pltpu.HBM)


def far_off(array):
    return pltpu.with_memory_space_constraint(array, pltpu.HBM)


def load_kernel(count, assign_ref, *refs):
    given, held, marks_ref, sems = refs[:count], refs[count : 2 * count], refs[-2], refs[-1]
    copies = [pltpu.make_async_copy(a, b, sems.at[n]) for n, (a, b) in enumerate(zip(given, held))]
    for copy in copies:
        copy.start()
    section = lax.axis_index("section")
    tokens = assign_ref.shape[0]
    row = lax.broadcasted_iota(jnp.int32, marks_ref.shape, 0)
    lane = lax.broadcasted_iota(jnp.int32, marks_ref.shape, 1)
    mark = jnp.full(marks_ref.shape, NOBODY, jnp.int32)
    for (wave, slot), at in SHORT.items():
        for token in range(tokens):
            low, high = [NOBODY if tick is None else assign_ref[token, tick] for tick in at]
            pick = jnp.where(section == 0, low, high)
            mark = jnp.where((row == slot * tokens + token) & (lane == wave), pick, mark)
    marks_ref[...] = mark.astype(jnp.float32)
    for copy in copies:
        copy.wait()


def load(assign, arrays):
    moved = sum(a.size * a.dtype.itemsize for a in arrays)
    marks = pltpu.VMEM((2 * assign.shape[0], LANES), jnp.float32)
    return pl.pallas_call(
        functools.partial(load_kernel, len(arrays)),
        out_shape=[pltpu.VMEM(a.shape, a.dtype) for a in arrays] + [marks],
        in_specs=[pl.BlockSpec(memory_space=pltpu.SMEM)] + [HBM] * len(arrays),
        out_specs=[WHOLE] * (len(arrays) + 1),
        scratch_shapes=[pltpu.SemaphoreType.DMA((len(arrays),))],
        compiler_params=small_limit(),
        cost_estimate=pl.CostEstimate(flops=0, bytes_accessed=2 * moved, transcendentals=0),
    )(assign, *[far_off(a) for a in arrays])


def stack_kernel(first_ref, second_ref, marks_ref, out_ref, wide_ref):
    tokens, width = first_ref.shape
    wide_ref[:tokens, :width] = first_ref[...].astype(jnp.float32)
    wide_ref[tokens:, :width] = second_ref[...].astype(jnp.float32)
    wide_ref[:, width:] = marks_ref[...]
    out_ref[...] = wide_ref[...].astype(out_ref.dtype)


def stack(first, second, marks):
    tokens, width = first.shape
    shape = (2 * tokens, width + LANES)
    return pl.pallas_call(
        stack_kernel,
        out_shape=pltpu.VMEM(shape, first.dtype),
        in_specs=[WHOLE] * 3,
        out_specs=WHOLE,
        scratch_shapes=[pltpu.VMEM(shape, jnp.float32)],
        compiler_params=small_limit(),
    )(near(first), near(second), near(marks))


def normalise(rows, gain_ref, table_ref, normed_ref, pick):
    square = jnp.mean(rows * rows, axis=-1, keepdims=True)
    normed = (rows * lax.rsqrt(square + EPSILON) * gain_ref[...]).astype(jnp.bfloat16)
    normed_ref[...] = normed
    wide = normed.astype(jnp.float32)
    table = table_ref[...].astype(jnp.float32)
    first = jnp.sum(wide * table[0:1], axis=-1, keepdims=True)
    second = jnp.sum(wide * table[1:2], axis=-1, keepdims=True)
    margin = jnp.where(pick < 0.5, first - second, second - first)
    return 1.0 / (1.0 + jnp.exp(-margin))


def nothing(*_):
    pass


def expert_rows(tiles, normed_ref, gate_ref, up_ref, down_ref, hidden_ref, pick, weight, wait=nothing):
    size = gate_ref.shape[1] // tiles
    for tile in range(tiles):
        at = slice(tile * size, (tile + 1) * size)
        gate = jnp.dot(normed_ref[...], gate_ref[:, at], preferred_element_type=jnp.float32)
        wait(0, tile)
        upper = jnp.dot(normed_ref[...], up_ref[:, at], preferred_element_type=jnp.float32)
        hidden_ref[:, at] = (gate / (1.0 + jnp.exp(-gate)) * upper).astype(jnp.bfloat16)
    size = down_ref.shape[1] // tiles
    mine = lax.axis_index("pair").astype(jnp.float32)
    for tile in range(tiles):
        at = slice(tile * size, (tile + 1) * size)
        wait(1, tile)
        part = jnp.dot(hidden_ref[...], down_ref[:, at], preferred_element_type=jnp.float32)
        chosen = jnp.broadcast_to(jnp.abs(pick - mine) < 0.5, part.shape)
        yield at, jnp.where(chosen, part * weight, 0.0)


def own_rows(shape, block):
    return lax.broadcasted_iota(jnp.int32, shape, 0) < block


def first_kernel(tiles, pieces, *refs):
    chunks, refs = refs[:pieces], refs[pieces:]
    gain_ref, table_ref, gate_ref, *given = refs[:5]
    own_ref, far_ref, marks_ref, *held = refs[5:10]
    rows_ref, normed_ref, hidden_ref, sems = refs[10:]

    def copy_of(n, tile):
        size = held[n].shape[1] // tiles
        at = pl.ds(tile * size, size)
        return pltpu.make_async_copy(given[n].at[:, at], held[n].at[:, at], sems.at[n, tile])

    for n in range(2):
        for tile in range(tiles):
            copy_of(n, tile).start()
    width = gain_ref.shape[1]
    start = 0
    for chunk in chunks:
        count = chunk.shape[0]
        rows_ref[start : start + count, :] = chunk[...].astype(jnp.float32)
        start += count
    marks_ref[...] = rows_ref[:, width:]
    pick = rows_ref[:, width : width + 1]
    weight = normalise(rows_ref[:, :width], gain_ref, table_ref, normed_ref, pick)
    half = start // 2
    parts = expert_rows(
        tiles, normed_ref, gate_ref, *held, hidden_ref, pick, weight, lambda n, tile: copy_of(n, tile).wait()
    )
    for at, part in parts:
        part = part + jnp.where(own_rows(part.shape, count), rows_ref[:, at], 0.0)
        part = part.astype(own_ref.dtype)
        own_ref[:, at] = part[:half]
        far_ref[:, at] = part[half:]


def expert_cost(rows, gate):
    return pl.CostEstimate(
        flops=6 * rows * gate.size, bytes_accessed=6 * gate.size, transcendentals=rows * gate.shape[1]
    )


def expert_scratch(rows, width, gate):
    return [
        pltpu.VMEM((rows, width), jnp.float32),
        pltpu.VMEM((rows, gate.shape[0]), jnp.bfloat16),
        pltpu.VMEM((rows, gate.shape[1]), jnp.bfloat16),
    ]


def first_call(chunks, gain, table, gate, up, down):
    rows, width = sum(chunk.shape[0] for chunk in chunks), gate.shape[0]
    tiles = tiles_of(*gate.shape)
    return pl.pallas_call(
        functools.partial(first_kernel, tiles, len(chunks)),
        out_shape=[pltpu.VMEM((rows // 2, width), gate.dtype)] * 2
        + [pltpu.VMEM((rows, LANES), jnp.float32)]
        + [pltpu.VMEM(w.shape, w.dtype) for w in (up, down)],
        in_specs=[WHOLE] * (len(chunks) + 3) + [HBM] * 2,
        out_specs=[WHOLE] * 5,
        scratch_shapes=expert_scratch(rows, width + LANES, gate) + [pltpu.SemaphoreType.DMA((2, tiles))],
        compiler_params=pltpu.CompilerParams(vmem_limit_bytes=12 << 20),
        cost_estimate=expert_cost(rows, gate),
    )(*[near(a) for a in (*chunks, gain, table, gate)], far_off(up), far_off(down))


def second_kernel(tiles, block, *refs):
    own_ref, far_ref, marks_ref, gain_ref, table_ref, gate_ref, up_ref, down_ref = refs[:8]
    out_ref, rows_ref, normed_ref, hidden_ref = refs[8:]
    half = own_ref.shape[0]
    rows_ref[:half, :] = own_ref[...].astype(jnp.float32)
    rows_ref[half:, :] = far_ref[...].astype(jnp.float32)
    pick = marks_ref[:, 1:2]
    weight = normalise(rows_ref[...], gain_ref, table_ref, normed_ref, pick)
    parts = expert_rows(tiles, normed_ref, gate_ref, up_ref, down_ref, hidden_ref, pick, weight)
    for at, part in parts:
        rows_ref[:, at] = part + jnp.where(own_rows(part.shape, block), rows_ref[:, at], 0.0)
    section, place, core = [lax.axis_index(name) for name in ("section", "expert", "pair")]
    shares, tokens, start = lax.axis_size("expert"), block // 2, 0
    for q in range(2):
        for share in range(shares):
            for slot in range(2):
                target = ((section ^ slot) * shares + (place ^ share)) * 2 + (core ^ q)
                out_ref[target] = rows_ref[start : start + tokens, :].astype(out_ref.dtype)
                start += tokens


def second_call(own, far, marks, gain, table, gate, up, down, block):
    rows, width = marks.shape[0], gate.shape[0]
    tokens = block // 2
    return pl.pallas_call(
        functools.partial(second_kernel, tiles_of(*gate.shape), block),
        out_shape=pltpu.VMEM((rows // tokens, tokens, width), own.dtype),
        in_specs=[WHOLE] * 8,
        out_specs=WHOLE,
        scratch_shapes=expert_scratch(rows, width, gate),
        compiler_params=pltpu.CompilerParams(vmem_limit_bytes=12 << 20),
        cost_estimate=expert_cost(rows, gate),
    )(*[near(a) for a in (own, far, marks, gain, table, gate, up, down)])


def sum_kernel(distances, block, *refs):
    pieces, out, total_ref = refs[: len(distances)], refs[-2], refs[-1]
    for n, (piece, distance) in enumerate(zip(pieces, distances)):
        value = piece[...].astype(jnp.float32)
        if distance:
            parts = [value[k * block : (k + 1) * block] for k in range(value.shape[0] // block)]
            for k in range(len(parts)):
                at = slice(k * block, (k + 1) * block)
                total_ref[at, :] = total_ref[at, :] + parts[k ^ distance]
        else:
            total_ref[...] = total_ref[...] + value if n else value
    out[...] = total_ref[...].astype(out.dtype)


def sum_of(pieces, distances, block):
    shape = pieces[0].shape
    return pl.pallas_call(
        functools.partial(sum_kernel, distances, block),
        out_shape=pltpu.VMEM(shape, pieces[0].dtype),
        in_specs=[WHOLE] * len(pieces),
        out_specs=WHOLE,
        scratch_shapes=[pltpu.VMEM(shape, jnp.float32)],
        compiler_params=small_limit(),
    )(*[near(piece) for piece in pieces])


def arrive_kernel(got_ref, inflight_ref, finished_ref):
    half = got_ref.shape[0] // 2
    for s, out in enumerate((inflight_ref, finished_ref)):
        total = got_ref[s * half].astype(jnp.float32)
        for n in range(1, half):
            total = total + got_ref[s * half + n].astype(jnp.float32)
        out[0] = total.astype(out.dtype)


def arrive(got):
    shape = jax.ShapeDtypeStruct((1,) + got.shape[1:], got.dtype)
    return pl.pallas_call(
        arrive_kernel,
        out_shape=[shape, shape],
        in_specs=[WHOLE],
        out_specs=[WHOLE, WHOLE],
        compiler_params=small_limit(),
    )(near(got))


def crossed(block, distance):
    shares = lax.axis_size("expert")
    route = [
        (s * shares + i, (1 - s) * shares + (i ^ distance)) for s in range(2) for i in range(shares)
    ]
    return lax.ppermute(block, ("section", "expert"), route)


def short_relay(transit, incoming, assign, gain, table, weights):
    shares, block = lax.axis_size("expert"), 2 * transit.shape[0]
    other = partner(incoming, "section", 1)
    transit, gain, table, gate, marks = load(assign, [transit, gain, table, weights[0]])
    packed = stack(transit, other, marks)
    near_by = spread(packed, "expert")
    chunks = near_by + [partner(chunk, "pair", 1) for chunk in near_by]
    own, far, marks, up, down = first_call(chunks, gain, table, gate, *weights[1:])
    total = sum_of([own, partner(far, "pair", 1)], [0, 0], block)
    total = sum_of([crossed(total, 0), crossed(total, 1)], [0, 1], block)
    distance = 2
    while distance < shares:
        total = sum_of([total, partner(total, "expert", distance)], [0, distance], block)
        distance *= 2
    far = partner(total, "pair", 1)
    parts = second_call(total, far, marks, gain, table, gate, up, down, block)
    return arrive(lax.all_to_all(parts, ("section", "expert", "pair"), 0, 0, tiled=True))


def is_short(ticks):
    shares = lax.axis_size("expert")
    few = not wide_axis("expert") and shares > 1 and shares & (shares - 1) == 0
    return lax.axis_size("section") == 2 and ticks == 3 and lax.axis_size("pair") == 2 and few


def body(
    transit_activation,
    incoming_queue,
    expert_assignment,
    rescale_factor,
    routing_matrix,
    gating_matrix,
    expand_matrix,
    contract_matrix,
):
    sections = lax.axis_size("section")
    ticks, tokens = expert_assignment.shape[1:3]
    table = routing_matrix[0].T
    assign = expert_assignment[0, :, :, 0].T
    weights = [w[0, 0] for w in (gating_matrix, expand_matrix, contract_matrix)]
    if is_short(ticks):
        return short_relay(
            transit_activation[0], incoming_queue[0], assign, rescale_factor, table, weights
        )
    reads, last, left = relay(sections, ticks)
    needs = {(source, job[0]) for job, source in reads.items()}
    needs |= {(value, s) for s, value in enumerate(last)}
    needs |= {(value, s) for s, value in enumerate(left)}
    store = Store(needs, tokens)
    store.add("incoming", incoming_queue[0], [[("incoming", s) for s in range(sections)]])
    store.add("transit", transit_activation[0], [[("transit", s) for s in range(sections)]])
    for number, wave in enumerate(waves_of(sections, ticks)):
        arrays, where = store.choices([[job and reads[job] for job in row] for row in wave])
        when = []
        for row in wave:
            options = {}
            for s, job in enumerate(row):
                if job:
                    options.setdefault(job[1], []).append(s)
            when.append(list(options.items()))
        packed = pack(arrays, where, when, assign, tokens)
        out, weights = layer(packed, rescale_factor, table, weights, number == 0)
        store.add(number, out, [[job and ("done",) + job for job in row] for row in wave])
    arrays, where = store.choices([last, left])
    return pick_out(arrays, [[options] for options in where], tokens)


def solution(mesh):
    in_specs = (
        P("section", ("groups", "expert", "pair"), None),
        P("section", ("groups", "expert", "pair"), None),
        P("section", None, ("groups", "expert", "pair"), None),
        P("section", None),
        P("section", None, None),
        P("section", "pair", None, "expert"),
        P("section", "pair", None, "expert"),
        P("section", "pair", "expert", None),
    )
    out_specs = (
        P("section", ("groups", "expert", "pair"), None),
        P("section", ("groups", "expert", "pair"), None),
    )
    return jax.shard_map(body, mesh=mesh, in_specs=in_specs, out_specs=out_specs, check_vma=False)
```
